512 devices in a mesh: shard: 128 (over y, z_hi, x), tensor: 4 (over z_lo, core).
Axes of the slice: x: 4, y: 8, z: 8 (z_hi: 4, z_lo: 2; z = z_hi * 2 + z_lo), core: 2. Of those that a mesh axis runs over, the one named last changes fastest.
Arguments:
- gradients: bfloat16 [128, 128, 32, 512], P('shard', None, 'tensor'), may hold values from -2 to 2
- master_weights: float32 [128, 32, 512], P('shard', 'tensor'), may hold values from -6 to 6
- first_moment: float32 [128, 32, 512], P('shard', 'tensor'), may hold values from -4 to 4
- second_moment: float32 [128, 32, 512], P('shard', 'tensor'), may hold values from 0.5 to 4
- old_basis: float32 [128, 512, 512], P('shard', 'tensor')
- old_stats: float32 [128, 512, 512], P('shard', 'tensor'), as said below
- owner_table: int32 [128], replicated, may hold values from 0 to 127, each once
Outputs:
- updated_weights: float32 [128, 32, 512], P(None, 'tensor')
- new_first: float32 [128, 32, 512], P('shard', 'tensor')
- new_second: float32 [128, 32, 512], P('shard', 'tensor')
- new_basis: float32 [128, 512, 512], P('shard', 'tensor')
- new_stats: float32 [128, 512, 512], P('shard', 'tensor')
The draws below stay inside these ranges and needn't reach their ends.
Inputs may be any that keep to these rules, and one draw needn't show every extreme that they name: owner_table names every owner 0 to 127 exactly once. `old_stats`: each block's matrix is symmetric.
All inputs are finite; a program needn't handle non-finite values.
Results may differ from the reference program's by a relative error of at most 0.004.
Values may be sent and summed in bfloat16 or wider, within the bound.
No kernel may reach another device: no remote copies, remote signals or barrier semaphores. Data moves between devices by JAX's collectives and lax.ppermute only.
A program may use at most 64 MiB of HBM per device.

```python
import math
import jax
import jax.numpy as jnp
from jax import lax

B = 512
NS_ITERS = 3
REPLICAS = 128
BLOCKS = 128
ROWS = 32
N_SHARD = 128


def draw_old_basis(key, part):
    noise_key = jax.random.fold_in(key, 11)
    noise = jnp.clip(jax.random.normal(noise_key, (BLOCKS, B, B), jnp.float32), -4.0, 4.0)
    diagonal = 0.7
    return diagonal * jnp.eye(B, dtype=jnp.float32)[None] + noise * (0.7 / math.sqrt(B))


def draw_old_stats(key, part):
    scale_key = jax.random.fold_in(key, 21)
    noise_key = jax.random.fold_in(key, 22)
    scales = jnp.exp(jax.random.uniform(scale_key, (BLOCKS, B), jnp.float32, math.log(2.0), math.log(40.0)))
    noise = jnp.clip(jax.random.normal(noise_key, (BLOCKS, B, B), jnp.float32), -4.0, 4.0)
    symmetric = (noise + jnp.swapaxes(noise, 1, 2)) * (0.5 / math.sqrt(2.0 * B))
    roots = jnp.sqrt(scales)
    return roots[:, :, None] * roots[:, None, :] * symmetric + scales[:, :, None] * jnp.eye(B, dtype=jnp.float32)[None]


def with_spikes(result, stream_key, source, target, blocks, factor):
    def block_of(axis_at):
        return (jnp.arange(result.shape[axis_at]) // (result.shape[axis_at] // blocks)).reshape((-1,) + (1,) * (result.ndim - 1 - axis_at))

    first = jax.random.permutation(stream_key, blocks)[block_of(target)]
    other_side = (block_of(target) + blocks // 2) % blocks
    return jnp.where((block_of(source) == first) | (block_of(source) == other_side), factor * result, result)


def levels(stream_key, shape, pieces, smallest, high):
    gain = 1.0
    for position, blocks in pieces:
        steps = jax.random.uniform(jax.random.fold_in(jax.random.fold_in(stream_key, 6), position), (blocks,), jnp.float32, smallest / len(pieces), high / len(pieces))
        gain = gain * jnp.repeat(jnp.exp(steps), shape[position] // blocks).reshape((-1,) + (1,) * (len(shape) - 1 - position))
    return gain


def normal_values(rng, extent, deviation, bound, pieces=(), kind=jnp.bfloat16):
    drawn = deviation * jax.random.normal(rng, extent, jnp.float32)
    if pieces:
        drawn = drawn * levels(rng, extent, pieces, -0.22, 0.18)
    return jnp.clip(drawn, -bound, bound).astype(kind)


def gaussian_with(own_key, dims, spread, limit, split, heavy, kind=jnp.bfloat16):
    drawn = spread * jax.random.normal(own_key, dims, jnp.float32)
    if split:
        drawn = drawn * levels(own_key, dims, split, -0.22, 0.18)
    return jnp.clip(with_spikes(drawn, jax.random.fold_in(own_key, 3), *heavy), -limit, limit).astype(kind)


def setup_inputs(seed: int = 0) -> dict:
    key_list = jax.random.split(jax.random.key(seed), 8)
    gradients = gaussian_with(key_list[0], (REPLICAS, BLOCKS, ROWS, B), N_SHARD ** -0.5, 2.0, ((0, 128), (2, 4)), (0, 1, 128, 5.5))
    master_weights = normal_values(key_list[1], (BLOCKS, ROWS, B), 1.0, 6.0, ((0, 128), (1, 4)), jnp.float32)
    first_moment = normal_values(key_list[2], (BLOCKS, ROWS, B), 0.5, 4.0, ((0, 128), (1, 4)), jnp.float32)
    second_moment = jnp.clip(jnp.exp(math.log(4.0) - 2.0794415 * jax.random.uniform(key_list[3], (BLOCKS, ROWS, B), jnp.float32) ** levels(key_list[3], (BLOCKS, ROWS, B), ((0, 128), (1, 4)), -0.2, 0.2)), 0.5, 4.0)
    old_basis = draw_old_basis(jax.random.fold_in(key_list[7], 71), 0)
    old_stats = draw_old_stats(jax.random.fold_in(key_list[7], 71), 0)
    owner_table = jax.random.permutation(key_list[6], BLOCKS).astype(jnp.int32)
    return {"gradients": gradients, "master_weights": master_weights, "first_moment": first_moment, "second_moment": second_moment, "old_basis": old_basis, "old_stats": old_stats, "owner_table": owner_table}


momentum_decay = 0.9
square_decay = 0.95
stats_decay = 0.95
step_size = 0.05
start_gain = 1.7
epsilon = 1e-06

def update_block(package):
    gradient, weight, first_old, second_old, basis_old, stats_old = package
    highest = lax.Precision.HIGHEST
    turned = jnp.dot(gradient, basis_old, precision=highest)
    first_new = momentum_decay * first_old + (1.0 - momentum_decay) * turned
    second_new = square_decay * second_old + (1.0 - square_decay) * turned * turned
    direction = first_new / jnp.sqrt(second_new)
    rotated_back = jnp.dot(direction, basis_old.T, precision=highest)
    weight_new = weight - step_size * rotated_back
    stats_new = stats_decay * stats_old + (1.0 - stats_decay) * jnp.dot(gradient.T, gradient, precision=highest)
    power = jnp.dot(stats_new, basis_old, precision=highest)
    squares = jnp.sum(power * power)
    iterate = power * (start_gain / jnp.sqrt(squares + epsilon))
    for sweep in range(NS_ITERS):
        gram_matrix = jnp.dot(iterate.T, iterate, precision=highest)
        iterate = 1.5 * iterate - 0.5 * jnp.dot(iterate, gram_matrix, precision=highest)
    return (weight_new, first_new, second_new, iterate, stats_new)

def reference(gradients, master_weights, first_moment, second_moment, old_basis, old_stats, owner_table):
    blocks = owner_table.shape[0]
    places = jnp.arange(blocks, dtype=jnp.int32)
    inverse = lax.optimization_barrier(jnp.sum(jnp.where(owner_table[None, :] == places[:, None], places[None, :], 0), axis=1)).astype(jnp.int32)
    summed = lax.optimization_barrier(jnp.sum(gradients, axis=0, dtype=jnp.float32))
    summed = jnp.take(summed, inverse, axis=0)
    weight_new, first_new, second_new, basis_new, stats_new = lax.map(update_block, (summed, master_weights, first_moment, second_moment, old_basis, old_stats))
    updated_weights = jnp.take(weight_new, owner_table, axis=0)
    return (updated_weights, first_new, second_new, basis_new, stats_new)
```

```python
import jax
import jax.numpy as jnp
from jax import lax
from jax.sharding import PartitionSpec as P

NS_ITERS = 3

momentum_decay = 0.9
square_decay = 0.95
stats_decay = 0.95
step_size = 0.05
start_gain = 1.7
epsilon = 1e-06

NY, NZ, NX = 8, 4, 4
NYZ = NY * NZ
NT = 4
X_GROUPS = [[yz * NX + x for x in range(NX)] for yz in range(NYZ)]
YZ_GROUPS = [[yz * NX + x for yz in range(NYZ)] for x in range(NX)]

HIGH = lax.Precision.HIGH


def exchange(value, groups):
    return lax.all_to_all(value, "shard", 0, 0, axis_index_groups=groups, tiled=True)


def swap(value, bit):
    return lax.ppermute(value, "tensor", [(t, t ^ bit) for t in range(NT)])


def gram_of(matrix):
    return lax.dot_general(matrix, matrix, (((0,), (0,)), ((), ())), precision=HIGH)


def body(gradients, master_weights, first_moment, second_moment, old_basis, old_stats, owner_table):
    blocks = owner_table.shape[0]
    rows, width = gradients.shape[2:]
    rows_here = old_basis.shape[1]
    tensor = lax.axis_index("tensor")
    core = tensor % 2

    own = jnp.concatenate([old_basis, old_stats])
    other = swap(own, 2)
    pair = jnp.where(tensor < 2, jnp.stack([own, other]), jnp.stack([other, own]))
    mate = swap(pair, 1)
    whole = jnp.where(core == 0, jnp.stack([pair, mate], 1), jnp.stack([mate, pair], 1))
    whole_basis = whole[:, :, 0].reshape(width, width)
    whole_stats = whole[:, :, 1].reshape(width, width)

    places = jnp.arange(blocks, dtype=jnp.int32)
    wanted = (places % NYZ) * NX + places // NYZ
    source = jnp.sum(
        jnp.where(owner_table[None, :] == wanted[:, None], places[None, :], 0), axis=1
    )
    ordered = jnp.take(gradients[0], source, axis=0, mode="clip")
    parts = exchange(ordered.reshape(NX, NYZ, rows, width), X_GROUPS)
    partial = jnp.sum(parts, axis=0, dtype=jnp.float32)
    summed = jnp.sum(exchange(partial, YZ_GROUPS), axis=0)

    turned = jnp.dot(summed, whole_basis, precision=HIGH)
    first_new = momentum_decay * first_moment[0] + (1.0 - momentum_decay) * turned
    second_new = square_decay * second_moment[0] + (1.0 - square_decay) * turned * turned
    direction = first_new / jnp.sqrt(second_new)
    rotated_back = lax.dot_general(
        direction, whole_basis, (((1,), (1,)), ((), ())), precision=HIGH
    )
    weight_new = master_weights[0] - step_size * rotated_back

    column = exchange(jnp.broadcast_to(weight_new, (NYZ, rows, width)), YZ_GROUPS)
    gathered = exchange(jnp.broadcast_to(column, (NX, NYZ, rows, width)), X_GROUPS)
    gathered = gathered.reshape(blocks, rows, width)
    updated_weights = jnp.take(gathered, (owner_table % NX) * NYZ + owner_table // NX, axis=0, mode="clip")

    whole_grad = lax.all_gather(summed, "tensor", axis=0, tiled=True)
    stats_new = stats_decay * whole_stats + (1.0 - stats_decay) * gram_of(whole_grad)
    position = tensor * rows_here
    own_stats = lax.dynamic_slice_in_dim(stats_new, position, rows_here, 0)
    power = jnp.dot(stats_new, whole_basis, precision=HIGH)
    gram_matrix = gram_of(power)
    factor = start_gain / jnp.sqrt(jnp.trace(gram_matrix) + epsilon)
    current = power * factor
    gram_matrix = gram_matrix * (factor * factor)
    for sweep in range(NS_ITERS):
        if sweep > 0:
            gram_matrix = gram_of(current)
        if sweep + 1 < NS_ITERS:
            current = 1.5 * current - 0.5 * jnp.dot(current, gram_matrix, precision=HIGH)
        else:
            own_rows = lax.dynamic_slice_in_dim(current, position, rows_here, 0)
            current = 1.5 * own_rows - 0.5 * jnp.dot(own_rows, gram_matrix, precision=HIGH)
    return (updated_weights, first_new[None], second_new[None], current[None], own_stats[None])


def solution(mesh):
    return jax.shard_map(
        body,
        mesh=mesh,
        in_specs=(
            P("shard", None, "tensor", None),
            P("shard", "tensor", None),
            P("shard", "tensor", None),
            P("shard", "tensor", None),
            P("shard", "tensor", None),
            P("shard", "tensor", None),
            P(),
        ),
        out_specs=(
            P(None, "tensor", None),
            P("shard", "tensor", None),
            P("shard", "tensor", None),
            P("shard", "tensor", None),
            P("shard", "tensor", None),
        ),
        check_vma=False,
    )
```

```python
import jax
import jax.numpy as jnp
from jax import lax
from jax.sharding import PartitionSpec as P

NS_ITERS = 3

momentum_decay = 0.9
square_decay = 0.95
stats_decay = 0.95
step_size = 0.05
start_gain = 1.7
epsilon = 1e-06

NY_HI, NY_LO, NZ, NX = 4, 2, 4, 4
NEAR, FAR = NY_LO * NX, NY_HI * NZ
NT = 4


def near_of(owner):
    return owner // (NX * NZ) % NY_LO * NX + owner % NX


def far_of(owner):
    return owner // (NX * NZ * NY_LO) * NZ + owner // NX % NZ


def owner_of(near, far):
    return ((far // NZ * NY_LO + near // NX) * NZ + far % NZ) * NX + near % NX


NEAR_GROUPS = [[owner_of(near, far) for near in range(NEAR)] for far in range(FAR)]
FAR_GROUPS = [[owner_of(near, far) for far in range(FAR)] for near in range(NEAR)]

HIGH = lax.Precision.HIGH


def exchange(value, groups):
    return lax.all_to_all(value, "shard", 0, 0, axis_index_groups=groups, tiled=True)


def swap(value, bit):
    return lax.ppermute(value, "tensor", [(t, t ^ bit) for t in range(NT)])


def gram_of(matrix):
    return lax.dot_general(matrix, matrix, (((0,), (0,)), ((), ())), precision=HIGH)


def body(gradients, master_weights, first_moment, second_moment, old_basis, old_stats, owner_table):
    blocks = owner_table.shape[0]
    rows, width = gradients.shape[2:]
    rows_here = old_basis.shape[1]
    tensor = lax.axis_index("tensor")
    core = tensor % 2

    places = jnp.arange(blocks, dtype=jnp.int32)
    wanted = owner_of(places // FAR, places % FAR)
    source = jnp.sum(
        jnp.where(owner_table[None, :] == wanted[:, None], places[None, :], 0), axis=1
    )
    ordered = jnp.take(gradients[0], source, axis=0, mode="clip")
    ordered, old_basis, old_stats = lax.optimization_barrier((ordered, old_basis, old_stats))
    parts = exchange(ordered.reshape(NEAR, FAR, rows, width), NEAR_GROUPS)
    partial = jnp.sum(parts, axis=0, dtype=jnp.float32)
    summed = jnp.sum(exchange(partial, FAR_GROUPS), axis=0)

    own = jnp.concatenate([old_basis, old_stats])
    other = swap(own, 2)
    pair = jnp.where(tensor < 2, jnp.stack([own, other]), jnp.stack([other, own]))
    mate = swap(pair, 1)
    whole = jnp.where(core == 0, jnp.stack([pair, mate], 1), jnp.stack([mate, pair], 1))
    whole_basis = whole[:, :, 0].reshape(width, width)
    whole_stats = whole[:, :, 1].reshape(width, width)

    turned = jnp.dot(summed, whole_basis, precision=HIGH)
    first_new = momentum_decay * first_moment[0] + (1.0 - momentum_decay) * turned
    second_new = square_decay * second_moment[0] + (1.0 - square_decay) * turned * turned
    direction = first_new / jnp.sqrt(second_new)
    rotated_back = lax.dot_general(
        direction, whole_basis, (((1,), (1,)), ((), ())), precision=HIGH
    )
    weight_new = master_weights[0] - step_size * rotated_back

    copies = jnp.broadcast_to(weight_new, (FAR, rows, width))
    copies, summed = lax.optimization_barrier((copies, summed))
    column = exchange(copies, FAR_GROUPS)
    largest = jnp.maximum(jnp.max(jnp.abs(column)), 2.0**-100)
    exponent = jnp.ceil(jnp.log2(largest))
    coded = (column * jnp.exp2(14.0 - exponent)).astype(jnp.float16)
    label = jnp.broadcast_to(exponent.astype(jnp.float16), (1, rows, width))
    coded = jnp.broadcast_to(jnp.concatenate([coded, label]), (NEAR, FAR + 1, rows, width))
    gathered = exchange(coded, NEAR_GROUPS)
    scales = jnp.exp2(gathered[:, FAR, 0, 0].astype(jnp.float32) - 14.0)
    near = near_of(owner_table)
    wide = jnp.take(
        gathered.reshape(NEAR * (FAR + 1), rows, width), near * (FAR + 1) + far_of(owner_table), axis=0, mode="clip"
    )
    scale = jnp.sum(jnp.where(near[:, None] == jnp.arange(NEAR)[None, :], scales[None, :], 0.0), axis=1)
    updated_weights = wide.astype(jnp.float32) * scale[:, None, None]

    whole_grad = lax.all_gather(summed, "tensor", axis=0, tiled=True)
    stats_new = stats_decay * whole_stats + (1.0 - stats_decay) * gram_of(whole_grad)
    position = tensor * rows_here
    own_stats = lax.dynamic_slice_in_dim(stats_new, position, rows_here, 0)
    power = jnp.dot(stats_new, whole_basis, precision=HIGH)
    gram_matrix = gram_of(power)
    factor = start_gain / jnp.sqrt(jnp.trace(gram_matrix) + epsilon)
    current = power * factor
    gram_matrix = gram_matrix * (factor * factor)
    for sweep in range(NS_ITERS):
        if sweep > 0:
            gram_matrix = gram_of(current)
        if sweep + 1 < NS_ITERS:
            current = 1.5 * current - 0.5 * jnp.dot(current, gram_matrix, precision=HIGH)
        else:
            own_rows = lax.dynamic_slice_in_dim(current, position, rows_here, 0)
            current = 1.5 * own_rows - 0.5 * jnp.dot(own_rows, gram_matrix, precision=HIGH)
    return (updated_weights, first_new[None], second_new[None], current[None], own_stats[None])


def solution(mesh):
    return jax.shard_map(
        body,
        mesh=mesh,
        in_specs=(
            P("shard", None, "tensor", None),
            P("shard", "tensor", None),
            P("shard", "tensor", None),
            P("shard", "tensor", None),
            P("shard", "tensor", None),
            P("shard", "tensor", None),
            P(),
        ),
        out_specs=(
            P(None, "tensor", None),
            P("shard", "tensor", None),
            P("shard", "tensor", None),
            P("shard", "tensor", None),
            P("shard", "tensor", None),
        ),
        check_vma=False,
    )
```

```python
import jax
import jax.numpy as jnp
from jax import lax
from jax.sharding import PartitionSpec as P


NS_ITERS = 3

momentum_decay = 0.9
square_decay = 0.95
stats_decay = 0.95
step_size = 0.05
start_gain = 1.7
epsilon = 1e-06

NY_HI, NY_LO, NZ, NX = 4, 2, 4, 4
NEAR, FAR = NY_LO * NX, NY_HI * NZ
NT = 4


def near_of(owner):
    return owner // (NX * NZ) % NY_LO * NX + owner % NX


def far_of(owner):
    return owner // (NX * NZ * NY_LO) * NZ + owner // NX % NZ


def owner_of(near, far):
    return ((far // NZ * NY_LO + near // NX) * NZ + far % NZ) * NX + near % NX


NEAR_GROUPS = [[owner_of(near, far) for near in range(NEAR)] for far in range(FAR)]
FAR_GROUPS = [[owner_of(near, far) for far in range(FAR)] for near in range(NEAR)]

HIGH = lax.Precision.HIGH


def exchange(value, groups):
    return lax.all_to_all(value, "shard", 0, 0, axis_index_groups=groups, tiled=True)


def swap(value, bit):
    return lax.ppermute(value, "tensor", [(t, t ^ bit) for t in range(NT)])


def gram_of(matrix):
    return lax.dot_general(matrix, matrix, (((0,), (0,)), ((), ())), precision=HIGH)


def step(gradients, master_weights, first_moment, second_moment, old_basis, old_stats, owner_table):
    blocks = owner_table.shape[0]
    rows, width = gradients.shape[2:]
    rows_here = old_basis.shape[1]
    tensor = lax.axis_index("tensor")
    core = tensor % 2

    places = jnp.arange(blocks, dtype=jnp.int32)
    wanted = owner_of(places // FAR, places % FAR)
    source = jnp.sum(
        jnp.where(owner_table[None, :] == wanted[:, None], places[None, :], 0), axis=1
    )
    ordered = jnp.take(gradients[0], source, axis=0, mode="clip")
    ordered, old_basis, old_stats = lax.optimization_barrier((ordered, old_basis, old_stats))
    parts = exchange(ordered.reshape(NEAR, FAR, rows, width), NEAR_GROUPS)
    partial = jnp.sum(parts, axis=0, dtype=jnp.float32)
    parts = exchange(partial, FAR_GROUPS)
    summed = jnp.sum(parts, axis=0)

    own = jnp.concatenate([old_basis, old_stats])
    other = swap(own, 2)
    pair = jnp.where(tensor < 2, jnp.stack([own, other]), jnp.stack([other, own]))
    mate = swap(pair, 1)
    whole = jnp.where(core == 0, jnp.stack([pair, mate], 1), jnp.stack([mate, pair], 1))
    whole_basis = whole[:, :, 0].reshape(width, width)
    decayed_stats = stats_decay * whole[:, :, 1].reshape(width, width)

    turned = jnp.dot(summed, whole_basis, precision=HIGH)
    first_new = momentum_decay * first_moment[0] + (1.0 - momentum_decay) * turned
    second_new = square_decay * second_moment[0] + (1.0 - square_decay) * turned * turned
    direction = first_new / jnp.sqrt(second_new)
    rotated_back = lax.dot_general(
        direction, whole_basis, (((1,), (1,)), ((), ())), precision=HIGH
    )
    weight_new = master_weights[0] - step_size * rotated_back

    copies = jnp.broadcast_to(weight_new, (FAR, rows, width))
    copies, summed = lax.optimization_barrier((copies, summed))
    column = exchange(copies, FAR_GROUPS)
    largest = jnp.maximum(jnp.max(jnp.abs(column)), 2.0**-100)
    exponent = jnp.ceil(jnp.log2(largest))
    coded = (column * jnp.exp2(14.0 - exponent)).astype(jnp.float16)
    label = jnp.broadcast_to(exponent.astype(jnp.float16), (1, rows, width))
    coded = jnp.broadcast_to(jnp.concatenate([coded, label]), (NEAR, FAR + 1, rows, width))
    gathered = exchange(coded, NEAR_GROUPS)
    scales = jnp.exp2(gathered[:, FAR, 0, 0].astype(jnp.float32) - 14.0)
    near = near_of(owner_table)
    wide = jnp.take(
        gathered.reshape(NEAR * (FAR + 1), rows, width), near * (FAR + 1) + far_of(owner_table), axis=0, mode="clip"
    )
    scale = jnp.sum(jnp.where(near[:, None] == jnp.arange(NEAR)[None, :], scales[None, :], 0.0), axis=1)
    updated_weights = wide.astype(jnp.float32) * scale[:, None, None]

    whole_grad = lax.all_gather(summed, "tensor", axis=0, tiled=True)
    stats_new = decayed_stats + (1.0 - stats_decay) * gram_of(whole_grad)
    position = tensor * rows_here
    own_stats = lax.dynamic_slice_in_dim(stats_new, position, rows_here, 0)
    power = jnp.dot(stats_new, whole_basis, precision=HIGH)
    gram_matrix = gram_of(power)
    factor = start_gain / jnp.sqrt(jnp.trace(gram_matrix) + epsilon)
    current = power * factor
    gram_matrix = gram_matrix * (factor * factor)
    for sweep in range(NS_ITERS):
        if sweep > 0:
            gram_matrix = gram_of(current)
        if sweep + 1 < NS_ITERS:
            current = 1.5 * current - 0.5 * jnp.dot(current, gram_matrix, precision=HIGH)
        else:
            own_rows = lax.dynamic_slice_in_dim(current, position, rows_here, 0)
            current = 1.5 * own_rows - 0.5 * jnp.dot(own_rows, gram_matrix, precision=HIGH)
    return (updated_weights, first_new[None], second_new[None], current[None], own_stats[None])


def solution(mesh):
    return jax.shard_map(
        step,
        mesh=mesh,
        in_specs=(
            P("shard", None, "tensor", None),
            P("shard", "tensor", None),
            P("shard", "tensor", None),
            P("shard", "tensor", None),
            P("shard", "tensor", None),
            P("shard", "tensor", None),
            P(),
        ),
        out_specs=(
            P(None, "tensor", None),
            P("shard", "tensor", None),
            P("shard", "tensor", None),
            P("shard", "tensor", None),
            P("shard", "tensor", None),
        ),
        check_vma=False,
    )
```
